32 devices in a mesh: dp: 1, ctx: 32 (over z, y, x, core).
Axes of the slice: x: 2, y: 2, z: 4, core: 2. Of those that a mesh axis runs over, the one named last changes fastest.
Arguments:
- queries: bfloat16 [4096, 8192], P(('dp', 'ctx')), may hold values from -16 to 16
- out_grad: bfloat16 [4096, 8192], P(('dp', 'ctx')), may hold values from -6 to 6
- enc_states: bfloat16 [384, 1024], P(('dp', 'ctx')), may hold values from -8 to 8
- w_key: bfloat16 [1024, 8192], P('dp', 'ctx'), may hold values from -1 to 1
- w_value: bfloat16 [1024, 8192], P('dp', 'ctx'), may hold values from -0.1875 to 0.1875
- dec_segments: int32 [4096], P(('dp', 'ctx')), may hold values from 0 to 3, as said below
- enc_segments: int32 [384], P(('dp', 'ctx')), may hold values from 0 to 3, as said below
Outputs:
- query_grad: bfloat16 [4096, 8192], P(('dp', 'ctx'))
- enc_grad: bfloat16 [384, 1024], P(('dp', 'ctx'))
- w_key_grad: float32 [1024, 8192], P('dp', 'ctx')
- w_value_grad: float32 [1024, 8192], P('dp', 'ctx')
The draws below stay inside these ranges and needn't reach their ends.
Inputs may be any that keep to these rules, and one draw needn't show every extreme that they name: `dec_segments`: within each pack the ids never fall along the tokens, and each of the 4 ids has one or more decoder tokens in the pack. `enc_segments`: within each pack the ids never fall along the tokens, and each of the 4 ids has two or more encoder tokens in the pack.
All inputs are finite; a program needn't handle non-finite values.
Results may differ from the reference program's by a relative error of at most 0.019.
Values may be sent and summed in bfloat16 or wider, within the bound.
A program may use at most 64 MiB of HBM per device.

```python
import math
import jax
import jax.numpy as jnp
from jax import lax

D = 1024
HEADS = 64
HEAD_DIM = 128
SEGS = 4
WIDTH = 8192
DEC_SEQ = 4096
ENC_SEQ = 384
PACKS = 1
DEC = 4096
ENC = 384
N_DP = 1


def segment_ids(seed_key, length, spacing):
    slot_count = length // spacing
    boundaries = (jax.random.permutation(seed_key, slot_count - 1)[:SEGS - 1] + 1) * spacing
    boundaries = jnp.sort(boundaries.astype(jnp.int32))
    positions = jnp.arange(length, dtype=jnp.int32)
    labels = jnp.sum((positions[:, None] >= boundaries[None, :]).astype(jnp.int32), axis=1)
    return (labels.astype(jnp.int32), boundaries)


def build(base_key):
    dec_keys = jax.random.split(jax.random.fold_in(base_key, 11), PACKS)
    enc_keys = jax.random.split(jax.random.fold_in(base_key, 12), PACKS)
    dec_ids, unused_bounds = jax.vmap(lambda item: segment_ids(item, DEC_SEQ, 1))(dec_keys)
    enc_ids, enc_bounds = jax.vmap(lambda item: segment_ids(item, ENC_SEQ, 2))(enc_keys)
    key_weight = jnp.clip(jax.random.normal(jax.random.fold_in(base_key, 13), (D, WIDTH), jnp.float32) / math.sqrt(D), -0.99, 0.99)
    encoder = jnp.clip(jax.random.normal(jax.random.fold_in(base_key, 14), (PACKS, ENC_SEQ, D), jnp.float32), -6.0, 6.0)
    queries = jnp.clip(0.09 * jax.random.normal(jax.random.fold_in(base_key, 15), (PACKS, DEC_SEQ, WIDTH), jnp.float32), -0.54, 0.54)
    return (queries, encoder, key_weight, dec_ids, enc_ids)


def draw_queries(key, part):
    return build(key)[0].reshape(DEC, WIDTH).astype(jnp.bfloat16)


def draw_enc_states(key, part):
    return build(key)[1].reshape(ENC, D).astype(jnp.bfloat16)


def draw_w_key(key, part):
    return build(key)[2].astype(jnp.bfloat16)


def draw_dec_segments(key, part):
    return build(key)[3].reshape(DEC).astype(jnp.int32)


def draw_enc_segments(key, part):
    return build(key)[4].reshape(ENC).astype(jnp.int32)


def block_scale(rng, shape, shards, least, largest):
    level, own = 1.0, jax.random.fold_in(rng, 6)
    for position, blocks in shards:
        draws = jnp.exp(jax.random.uniform(jax.random.fold_in(own, position), (blocks,), jnp.float32, least / len(shards), largest / len(shards)))
        level = level * jnp.repeat(draws, shape[position] // blocks).reshape([-1 if axis == position else 1 for axis in range(len(shape))])
    return level


def noise(own_key, extent, spread, reach, cuts=(), held_as=jnp.bfloat16):
    level = block_scale(own_key, extent, cuts, -0.22, 0.18) if cuts else 1.0
    values = jax.random.normal(own_key, extent, jnp.float32) * spread * level
    return jnp.minimum(jnp.maximum(values, -reach), reach).astype(held_as)


def setup_inputs(seed: int = 0) -> dict:
    keys = jax.random.split(jax.random.key(seed), 8)
    queries = draw_queries(jax.random.fold_in(keys[7], 71), 0)
    out_grad = noise(keys[1], (DEC, WIDTH), 1.0, 6.0, ((0, 32),))
    enc_states = draw_enc_states(jax.random.fold_in(keys[7], 71), 0)
    w_key = draw_w_key(jax.random.fold_in(keys[7], 71), 0)
    w_value = noise(keys[4], (D, WIDTH), D ** -0.5, 0.1875, ((1, 32),))
    dec_segments = draw_dec_segments(jax.random.fold_in(keys[7], 71), 0)
    enc_segments = draw_enc_segments(jax.random.fold_in(keys[7], 71), 0)
    return {"queries": queries, "out_grad": out_grad, "enc_states": enc_states, "w_key": w_key, "w_value": w_value, "dec_segments": dec_segments, "enc_segments": enc_segments}


def pack_grads(queries, out_grads, key_rows, value_rows, query_ids, key_ids):
    length = queries.shape[0]
    key_count = key_rows.shape[0]
    group_size = 4 if HEADS % 4 == 0 else 1
    column_count = group_size * HEAD_DIM
    allowed = query_ids[:, None] == key_ids[None, :]

    def head_group(number):
        column_start = number * column_count

        def slice_heads(source, count):
            piece = lax.dynamic_slice_in_dim(source, column_start, column_count, 1)
            return piece.reshape(count, group_size, HEAD_DIM).astype(jnp.float32)

        query_block = slice_heads(queries, length)
        grad_block = slice_heads(out_grads, length)
        key_block = slice_heads(key_rows, key_count)
        value_block = slice_heads(value_rows, key_count)
        scores = jnp.einsum("qhd,khd->hqk", query_block, key_block)
        scores = jnp.where(allowed[None], scores, -jnp.inf)
        highest = jnp.max(scores, axis=2, keepdims=True)
        weights = jnp.exp(scores - highest)
        probability = weights / jnp.sum(weights, axis=2, keepdims=True)
        rounded = lax.optimization_barrier(probability.astype(jnp.bfloat16)).astype(jnp.float32)
        upstream = jnp.einsum("qhd,khd->hqk", grad_block, value_block)
        row_dot = jnp.sum(probability * upstream, axis=2, keepdims=True)
        score_grad = lax.optimization_barrier((probability * (upstream - row_dot)).astype(jnp.bfloat16)).astype(jnp.float32)
        query_grad = jnp.einsum("hqk,khd->qhd", score_grad, key_block).astype(jnp.bfloat16)
        key_grad = jnp.einsum("hqk,qhd->khd", score_grad, query_block)
        value_grad = jnp.einsum("hqk,qhd->khd", rounded, grad_block)
        return (query_grad.reshape(length, column_count), key_grad.reshape(key_count, column_count), value_grad.reshape(key_count, column_count))

    pieces = lax.map(head_group, jnp.arange(HEADS // group_size, dtype=jnp.int32))
    return tuple(jnp.moveaxis(piece, 0, 1).reshape(piece.shape[1], HEADS * HEAD_DIM) for piece in pieces)


def reference(queries, out_grad, enc_states, w_key, w_value, dec_segments, enc_segments):
    full_width = HEADS * HEAD_DIM
    key_all = jnp.dot(enc_states, w_key, preferred_element_type=jnp.float32).astype(jnp.bfloat16)
    value_all = jnp.dot(enc_states, w_value, preferred_element_type=jnp.float32).astype(jnp.bfloat16)
    stacked = (queries.reshape(N_DP, DEC_SEQ, full_width), out_grad.reshape(N_DP, DEC_SEQ, full_width), key_all.reshape(N_DP, ENC_SEQ, full_width), value_all.reshape(N_DP, ENC_SEQ, full_width), dec_segments.reshape(N_DP, DEC_SEQ), enc_segments.reshape(N_DP, ENC_SEQ))

    def one_pack(packed):
        return pack_grads(packed[0], packed[1], packed[2], packed[3], packed[4], packed[5])

    query_grad, key_grad, value_grad = lax.map(one_pack, stacked)
    query_grad = query_grad.reshape(DEC, full_width)
    key_round = key_grad.reshape(ENC, full_width).astype(jnp.bfloat16)
    value_round = value_grad.reshape(ENC, full_width).astype(jnp.bfloat16)
    enc_grad = (jnp.dot(key_round, w_key.T, preferred_element_type=jnp.float32) + jnp.dot(value_round, w_value.T, preferred_element_type=jnp.float32)).astype(jnp.bfloat16)
    w_key_grad = jnp.dot(enc_states.T, key_round, preferred_element_type=jnp.float32)
    w_value_grad = jnp.dot(enc_states.T, value_round, preferred_element_type=jnp.float32)
    return query_grad, enc_grad, w_key_grad, w_value_grad
```

```python
import functools

import jax
import jax.numpy as jnp
from jax import lax
from jax.experimental import pallas as pl
from jax.experimental.pallas import tpu as pltpu
from jax.sharding import PartitionSpec as P

HEAD_DIM = 128
MESH = pl.DeviceIdType.MESH
ROWS = 16


def flipped(j, s, group):
    result, weight = 0, 1
    while weight < group:
        result = result + weight * (((j // weight) + (s // weight)) % 2)
        weight *= 2
    return result


def kernel(
    planes, group, q_hbm, g_hbm, qid_ref, encx_ref, wk_ref, wv_ref, sel_ref,
    dq_out, kr_out, enc_out, eg_out,
    encbuf, qbuf, gbuf, qids, kv, kids, dqbuf, acc, own, rs_send, rs_recv,
    eg_send, eg_recv, eg2_send, eg2_recv,
    enc1_s, enc1_r, enc2_s, enc2_r, qid_s, qid_r, q_s, q_r, g_s, g_r,
    kv_s, kv_r, dq_s, dq_r, rs_s, rs_r, eg_s, eg_r, eg2_s, eg2_r,
):
    me = lax.axis_index("ctx")
    z, j = me // group, me % group
    tokens = q_hbm.shape[0]
    width = wk_ref.shape[1]
    depth = wk_ref.shape[0]
    f32, bf16 = jnp.float32, jnp.bfloat16

    def send(src, dst, s_sem, r_sem, plane, member):
        return pltpu.make_async_remote_copy(
            src_ref=src, dst_ref=dst, send_sem=s_sem, recv_sem=r_sem,
            device_id={"ctx": plane * group + member}, device_id_type=MESH,
        )

    def arrive(ref, sem):
        pltpu.make_async_copy(ref, ref, sem).wait()

    barrier = pltpu.get_barrier_semaphore()
    for s in range(1, group):
        pl.semaphore_signal(
            barrier, inc=1, device_id={"ctx": z * group + flipped(j, s, group)}, device_id_type=MESH
        )
    for d in range(1, planes):
        pl.semaphore_signal(
            barrier, inc=1, device_id={"ctx": ((z + d) % planes) * group + j}, device_id_type=MESH
        )
    pl.semaphore_wait(barrier, group - 1 + planes - 1)

    for d in range(1, planes):
        send(encx_ref, encbuf.at[z, j], enc1_s.at[d], enc1_r.at[z], (z + d) % planes, j).start()
    encbuf[z, j] = encx_ref[...]
    qids[j] = qid_ref[...]
    for d in range(1, planes):
        other = (z + d) % planes
        arrive(encbuf.at[other, j], enc1_r.at[other])
    for s in range(1, group):
        p = flipped(j, s, group)
        send(encbuf.at[:, j], encbuf.at[:, j], enc2_s.at[s], enc2_r.at[j], z, p).start()
        send(qid_ref, qids.at[j], qid_s.at[s], qid_r.at[j], z, p).start()

    def columns(zb, p):
        return pl.ds(pl.multiple_of((zb * group + p) * width, width), width)

    def launch(d, carry):
        zb = (z + d) % planes

        def to_peer(s, c):
            p = flipped(j, s, group)
            cols = columns(zb, p)
            send(q_hbm.at[:, cols], qbuf.at[zb, j], q_s.at[zb, p], q_r.at[zb, j], z, p).start()
            send(g_hbm.at[:, cols], gbuf.at[zb, j], g_s.at[zb, p], g_r.at[zb, j], z, p).start()
            return c

        pltpu.make_async_copy(q_hbm.at[:, columns(zb, j)], qbuf.at[zb, j], q_r.at[zb, j]).start()
        pltpu.make_async_copy(g_hbm.at[:, columns(zb, j)], gbuf.at[zb, j], g_r.at[zb, j]).start()
        return lax.fori_loop(1, group, to_peer, carry)

    lax.fori_loop(0, planes, launch, 0)

    for s in range(1, group):
        p = flipped(j, s, group)
        arrive(encbuf.at[:, p], enc2_r.at[p])
        arrive(qids.at[p], qid_r.at[p])
    rows = planes * group * ROWS
    encoder = encbuf[...].reshape(rows, encbuf.shape[-1])
    enc_out[...] = encoder[:, :depth]
    selector = sel_ref[...]
    key_pad = jnp.dot(encoder[:, :depth], wk_ref[...], preferred_element_type=f32).astype(bf16)
    value_pad = jnp.dot(encoder[:, :depth], wv_ref[...], preferred_element_type=f32).astype(bf16)
    kv[z, :, :width] = jnp.dot(selector, key_pad, preferred_element_type=f32).astype(bf16)
    kv[z, :, width:] = jnp.dot(selector, value_pad, preferred_element_type=f32).astype(bf16)
    kids[...] = jnp.dot(selector, encoder[:, depth:], preferred_element_type=f32)
    for d in range(1, planes):
        send(kv.at[z], kv.at[z], kv_s.at[d], kv_r.at[z], (z + planes - d) % planes, j).start()

    heads = width // HEAD_DIM
    over_rows = (((0,), (0,)), ((), ()))
    over_cols = (((1,), (1,)), ((), ()))

    def column_step(d, carry):
        zb = (z + d) % planes

        @pl.when(d > 0)
        def _():
            arrive(kv.at[zb], kv_r.at[zb])

        acc[...] = jnp.zeros_like(acc)

        def member_step(s, c):
            p = flipped(j, s, group)
            arrive(qbuf.at[zb, p], q_r.at[zb, p])
            arrive(gbuf.at[zb, p], g_r.at[zb, p])
            allowed = kids[...] == qids[p][0:1, :]
            for h in range(heads):
                lo, hi = h * HEAD_DIM, (h + 1) * HEAD_DIM
                key = kv[zb, :, lo:hi]
                value = kv[zb, :, width + lo : width + hi]
                query = qbuf[zb, p, :, lo:hi]
                grad = gbuf[zb, p, :, lo:hi]
                scores = lax.dot_general(key, query, over_cols, preferred_element_type=f32)
                scores = jnp.where(allowed, scores, -jnp.inf)
                weights = jnp.exp(scores - jnp.max(scores, axis=0, keepdims=True))
                prob = weights * (1.0 / jnp.sum(weights, axis=0, keepdims=True))
                upstream = lax.dot_general(value, grad, over_cols, preferred_element_type=f32)
                row_dot = jnp.sum(prob * upstream, axis=0, keepdims=True)
                score_grad = (prob * (upstream - row_dot)).astype(bf16)
                acc[:, lo:hi] += jnp.dot(score_grad, query, preferred_element_type=f32)
                acc[:, width + lo : width + hi] += jnp.dot(
                    prob.astype(bf16), grad, preferred_element_type=f32
                )
                dqbuf[zb, p, :, lo:hi] = lax.dot_general(
                    score_grad, key, over_rows, preferred_element_type=f32
                ).astype(bf16)

            @pl.when(s > 0)
            def _():
                send(dqbuf.at[zb, p], dq_out.at[j, zb], dq_s.at[zb, p], dq_r.at[zb, j], z, p).start()

            @pl.when(s == 0)
            def _():
                pltpu.make_async_copy(dqbuf.at[zb, p], dq_out.at[j, zb], dq_r.at[zb, j]).start()

            return c

        lax.fori_loop(0, group, member_step, 0)

        @pl.when(d == 0)
        def _():
            own[...] = acc[...]

        @pl.when(d > 0)
        def _():
            rs_send[zb] = acc[...].astype(bf16)
            send(rs_send.at[zb], rs_recv.at[z], rs_s.at[zb], rs_r.at[z], zb, j).start()

        return carry

    lax.fori_loop(0, planes, column_step, 0)

    for d in range(1, planes):
        other = (z + d) % planes
        arrive(rs_recv.at[other], rs_r.at[other])
        own[...] += rs_recv[other].astype(f32)
    total = own[...].astype(bf16)
    spread = lax.dot_general(selector, total, over_rows, preferred_element_type=f32).astype(bf16)
    kr_out[...] = spread
    for zd in range(planes):
        part = spread[zd * group * ROWS : (zd + 1) * group * ROWS]
        eg_send[zd] = (
            lax.dot_general(part[:, :width], wk_ref[...], over_cols, preferred_element_type=f32)
            + lax.dot_general(part[:, width:], wv_ref[...], over_cols, preferred_element_type=f32)
        ).astype(bf16)

    def member_rows(p):
        return eg_send.at[:, pl.ds(pl.multiple_of(p * ROWS, ROWS), ROWS), :]

    for s in range(1, group):
        p = flipped(j, s, group)
        send(member_rows(p), eg_recv.at[j], eg_s.at[p], eg_r.at[j], z, p).start()
    term = member_rows(j)[...].astype(f32)
    for s in range(1, group):
        p = flipped(j, s, group)
        arrive(eg_recv.at[p], eg_r.at[p])
        term = term + eg_recv[p].astype(f32)
    eg2_send[...] = term.astype(bf16)
    for d in range(1, planes):
        other = (z + d) % planes
        send(eg2_send.at[other], eg2_recv.at[z], eg2_s.at[other], eg2_r.at[z], other, j).start()
    final = eg2_send[z].astype(f32)
    for d in range(1, planes):
        other = (z + d) % planes
        arrive(eg2_recv.at[other], eg2_r.at[other])
        final = final + eg2_recv[other].astype(f32)
    eg_out[...] = final.astype(bf16)

    for d in range(1, planes):
        other = (z + d) % planes
        arrive(encx_ref, enc1_s.at[d])
        arrive(kv.at[z], kv_s.at[d])
        arrive(rs_send.at[other], rs_s.at[other])
        arrive(eg2_send.at[other], eg2_s.at[other])
    for s in range(1, group):
        p = flipped(j, s, group)
        arrive(encbuf.at[:, j], enc2_s.at[s])
        arrive(qid_ref, qid_s.at[s])
        arrive(member_rows(p), eg_s.at[p])

    def drain(d, carry):
        def peer(s, c):
            p = flipped(j, s, group)
            arrive(qbuf.at[d, p], q_s.at[d, p])
            arrive(gbuf.at[d, p], g_s.at[d, p])
            arrive(dqbuf.at[d, p], dq_s.at[d, p])
            arrive(dq_out.at[p, d], dq_r.at[d, p])
            return c

        arrive(dq_out.at[j, d], dq_r.at[d, j])
        return lax.fori_loop(1, group, peer, carry)

    lax.fori_loop(0, planes, drain, 0)


def body(n, queries, out_grad, enc_states, w_key, w_value, dec_segments, enc_segments):
    key_weight = lax.all_gather(w_key, "dp", axis=0, tiled=True)
    value_weight = lax.all_gather(w_value, "dp", axis=0, tiled=True)
    bf16, f32 = jnp.bfloat16, jnp.float32
    group = 8 if n % 8 == 0 else 1
    planes = n // group
    tokens = queries.shape[0]
    own_rows, depth = enc_states.shape
    width = key_weight.shape[1]
    keys = n * own_rows
    padded = n * ROWS
    ids = jnp.broadcast_to(enc_segments.astype(bf16)[:, None], (own_rows, tokens))
    encx = jnp.pad(jnp.concatenate([enc_states, ids], axis=1), ((0, ROWS - own_rows), (0, 0)))
    qid = jnp.broadcast_to(dec_segments.astype(f32)[None, :], (8, tokens))
    row = jnp.arange(keys, dtype=jnp.int32)
    place = row // own_rows * ROWS + row % own_rows
    selector = (place[:, None] == jnp.arange(padded, dtype=jnp.int32)[None, :]).astype(bf16)
    vm = pl.BlockSpec(memory_space=pltpu.VMEM)
    hbm = pl.BlockSpec(memory_space=pl.ANY)
    dma = pltpu.SemaphoreType.DMA
    pairs = (planes, group)
    dq, spread, encoder, enc_grad = pl.pallas_call(
        functools.partial(kernel, planes, group),
        out_shape=(
            jax.ShapeDtypeStruct((group, planes, tokens, width), bf16),
            jax.ShapeDtypeStruct((padded, 2 * width), bf16),
            jax.ShapeDtypeStruct((padded, depth), bf16),
            jax.ShapeDtypeStruct((ROWS, depth), bf16),
        ),
        in_specs=[hbm, hbm, vm, vm, vm, vm, vm],
        out_specs=(hbm, vm, vm, vm),
        scratch_shapes=[
            pltpu.VMEM((planes, group, ROWS, depth + tokens), bf16),
            pltpu.VMEM((planes, group, tokens, width), bf16),
            pltpu.VMEM((planes, group, tokens, width), bf16),
            pltpu.VMEM((group, 8, tokens), f32),
            pltpu.VMEM((planes, keys, 2 * width), bf16),
            pltpu.VMEM((keys, tokens), f32),
            pltpu.VMEM((planes, group, tokens, width), bf16),
            pltpu.VMEM((keys, 2 * width), f32),
            pltpu.VMEM((keys, 2 * width), f32),
            pltpu.VMEM((planes, keys, 2 * width), bf16),
            pltpu.VMEM((planes, keys, 2 * width), bf16),
            pltpu.VMEM((planes, group * ROWS, depth), bf16),
            pltpu.VMEM((group, planes, ROWS, depth), bf16),
            pltpu.VMEM((planes, ROWS, depth), bf16),
            pltpu.VMEM((planes, ROWS, depth), bf16),
            dma((planes,)), dma((planes,)), dma((group,)), dma((group,)),
            dma((group,)), dma((group,)),
            dma(pairs), dma(pairs), dma(pairs), dma(pairs),
            dma((planes,)), dma((planes,)), dma(pairs), dma(pairs),
            dma((planes,)), dma((planes,)), dma((group,)), dma((group,)),
            dma((planes,)), dma((planes,)),
        ],
        compiler_params=pltpu.CompilerParams(
            collective_id=0, has_side_effects=True, vmem_limit_bytes=48 * 1024 * 1024
        ),
    )(queries, out_grad, qid, encx, key_weight, value_weight, selector)
    query_grad = jnp.transpose(dq, (2, 1, 0, 3)).reshape(tokens, n * width)
    down = (((0,), (0,)), ((), ()))
    grads = []
    for first in (0, width):
        term = lax.dot_general(
            encoder, spread[:, first : first + width], down, preferred_element_type=f32
        )
        if lax.axis_size("dp") > 1:
            term = lax.psum_scatter(
                term.astype(bf16), "dp", scatter_dimension=0, tiled=True
            ).astype(f32)
        grads.append(term)
    return query_grad, enc_grad[:own_rows], grads[0], grads[1]


def solution(mesh):
    both = ("dp", "ctx")
    in_specs = (
        P(both, None), P(both, None), P(both, None), P("dp", "ctx"), P("dp", "ctx"), P(both), P(both),
    )
    out_specs = (P(both, None), P(both, None), P("dp", "ctx"), P("dp", "ctx"))
    return jax.shard_map(
        functools.partial(body, mesh.shape["ctx"]),
        mesh=mesh, in_specs=in_specs, out_specs=out_specs, check_vma=False,
    )
```

```python
import functools

import jax
import jax.numpy as jnp
from jax import lax
from jax.experimental import pallas as pl
from jax.experimental.pallas import tpu as pltpu
from jax.sharding import PartitionSpec as P

HEAD_DIM = 128
MESH = pl.DeviceIdType.MESH
ROWS = 16


def flipped(j, s, group):
    result, weight = 0, 1
    while weight < group:
        result = result + weight * (((j // weight) + (s // weight)) % 2)
        weight *= 2
    return result


def kernel(
    planes, group, q_hbm, g_hbm, qid_ref, encx_ref, wk_hbm, wv_hbm, sel_hbm,
    dq_out, kr_out, enc_out, eg_out,
    wk_ref, wv_ref, sel_ref, w_sem, encbuf, qbuf, gbuf, qids, kv, kids, dqbuf, acc, own, rs_send, rs_recv,
    eg_send, eg_recv, eg2_send, eg2_recv,
    enc1_s, enc1_r, enc2_s, enc2_r, qid_s, qid_r, q_s, q_r, g_s, g_r,
    kv_s, kv_r, dq_s, dq_r, rs_s, rs_r, eg_s, eg_r, eg2_s, eg2_r,
):
    me = lax.axis_index("ctx")
    z, j = me // group, me % group
    tokens = q_hbm.shape[0]
    width = wk_ref.shape[1]
    depth = wk_ref.shape[0]
    f32, bf16 = jnp.float32, jnp.bfloat16

    def send(src, dst, s_sem, r_sem, plane, member):
        return pltpu.make_async_remote_copy(
            src_ref=src, dst_ref=dst, send_sem=s_sem, recv_sem=r_sem,
            device_id={"ctx": plane * group + member}, device_id_type=MESH,
        )

    def arrive(ref, sem):
        pltpu.make_async_copy(ref, ref, sem).wait()

    loads = [
        pltpu.make_async_copy(src, dst, w_sem.at[i])
        for i, (src, dst) in enumerate(((wk_hbm, wk_ref), (wv_hbm, wv_ref), (sel_hbm, sel_ref)))
    ]
    for load in loads:
        load.start()
    barrier = pltpu.get_barrier_semaphore()
    for s in range(1, group):
        pl.semaphore_signal(
            barrier, inc=1, device_id={"ctx": z * group + flipped(j, s, group)}, device_id_type=MESH
        )
    for d in range(1, planes):
        pl.semaphore_signal(
            barrier, inc=1, device_id={"ctx": ((z + d) % planes) * group + j}, device_id_type=MESH
        )
    pl.semaphore_wait(barrier, group - 1 + planes - 1)

    for d in range(1, planes):
        send(encx_ref, encbuf.at[z, j], enc1_s.at[d], enc1_r.at[z], (z + d) % planes, j).start()
    encbuf[z, j] = encx_ref[...]
    qids[j] = qid_ref[...]
    for d in range(1, planes):
        other = (z + d) % planes
        arrive(encbuf.at[other, j], enc1_r.at[other])
    for s in range(1, group):
        p = flipped(j, s, group)
        send(encbuf.at[:, j], encbuf.at[:, j], enc2_s.at[s], enc2_r.at[j], z, p).start()
        send(qid_ref, qids.at[j], qid_s.at[s], qid_r.at[j], z, p).start()

    def columns(zb, p):
        return pl.ds(pl.multiple_of((zb * group + p) * width, width), width)

    def launch(d, carry):
        zb = (z + d) % planes

        def to_peer(s, c):
            p = flipped(j, s, group)
            cols = columns(zb, p)
            send(q_hbm.at[:, cols], qbuf.at[zb, j], q_s.at[zb, p], q_r.at[zb, j], z, p).start()
            send(g_hbm.at[:, cols], gbuf.at[zb, j], g_s.at[zb, p], g_r.at[zb, j], z, p).start()
            return c

        pltpu.make_async_copy(q_hbm.at[:, columns(zb, j)], qbuf.at[zb, j], q_r.at[zb, j]).start()
        pltpu.make_async_copy(g_hbm.at[:, columns(zb, j)], gbuf.at[zb, j], g_r.at[zb, j]).start()
        return lax.fori_loop(1, group, to_peer, carry)

    lax.fori_loop(0, planes, launch, 0)

    for s in range(1, group):
        p = flipped(j, s, group)
        arrive(encbuf.at[:, p], enc2_r.at[p])
        arrive(qids.at[p], qid_r.at[p])
    for load in loads:
        load.wait()
    rows = planes * group * ROWS
    encoder = encbuf[...].reshape(rows, encbuf.shape[-1])
    enc_out[...] = encoder[:, :depth]
    selector = sel_ref[...]
    key_pad = jnp.dot(encoder[:, :depth], wk_ref[...], preferred_element_type=f32).astype(bf16)
    value_pad = jnp.dot(encoder[:, :depth], wv_ref[...], preferred_element_type=f32).astype(bf16)
    kv[z, :, :width] = jnp.dot(selector, key_pad, preferred_element_type=f32).astype(bf16)
    kv[z, :, width:] = jnp.dot(selector, value_pad, preferred_element_type=f32).astype(bf16)
    kids[...] = jnp.dot(selector, encoder[:, depth:], preferred_element_type=f32)
    for d in range(1, planes):
        send(kv.at[z], kv.at[z], kv_s.at[d], kv_r.at[z], (z + planes - d) % planes, j).start()

    heads = width // HEAD_DIM
    over_rows = (((0,), (0,)), ((), ()))
    over_cols = (((1,), (1,)), ((), ()))

    def column_step(d, carry):
        zb = (z + d) % planes

        @pl.when(d > 0)
        def _():
            arrive(kv.at[zb], kv_r.at[zb])

        acc[...] = jnp.zeros_like(acc)

        def member_step(s, c):
            p = flipped(j, s, group)
            arrive(qbuf.at[zb, p], q_r.at[zb, p])
            arrive(gbuf.at[zb, p], g_r.at[zb, p])
            allowed = kids[...] == qids[p][0:1, :]
            for h in range(heads):
                lo, hi = h * HEAD_DIM, (h + 1) * HEAD_DIM
                key = kv[zb, :, lo:hi]
                value = kv[zb, :, width + lo : width + hi]
                query = qbuf[zb, p, :, lo:hi]
                grad = gbuf[zb, p, :, lo:hi]
                scores = lax.dot_general(key, query, over_cols, preferred_element_type=f32)
                scores = jnp.where(allowed, scores, -jnp.inf)
                weights = jnp.exp(scores - jnp.max(scores, axis=0, keepdims=True))
                prob = weights * (1.0 / jnp.sum(weights, axis=0, keepdims=True))
                upstream = lax.dot_general(value, grad, over_cols, preferred_element_type=f32)
                row_dot = jnp.sum(prob * upstream, axis=0, keepdims=True)
                score_grad = (prob * (upstream - row_dot)).astype(bf16)
                acc[:, lo:hi] += jnp.dot(score_grad, query, preferred_element_type=f32)
                acc[:, width + lo : width + hi] += jnp.dot(
                    prob.astype(bf16), grad, preferred_element_type=f32
                )
                dqbuf[zb, p, :, lo:hi] = lax.dot_general(
                    score_grad, key, over_rows, preferred_element_type=f32
                ).astype(bf16)

            @pl.when(s > 0)
            def _():
                send(dqbuf.at[zb, p], dq_out.at[:, columns(zb, j)], dq_s.at[zb, p], dq_r.at[zb, j], z, p).start()

            @pl.when(s == 0)
            def _():
                pltpu.make_async_copy(dqbuf.at[zb, p], dq_out.at[:, columns(zb, j)], dq_r.at[zb, j]).start()

            return c

        lax.fori_loop(0, group, member_step, 0)

        @pl.when(d == 0)
        def _():
            own[...] = acc[...]

        @pl.when(d > 0)
        def _():
            rs_send[zb] = acc[...].astype(bf16)
            send(rs_send.at[zb], rs_recv.at[z], rs_s.at[zb], rs_r.at[z], zb, j).start()

        return carry

    lax.fori_loop(0, planes, column_step, 0)

    for d in range(1, planes):
        other = (z + d) % planes
        arrive(rs_recv.at[other], rs_r.at[other])
        own[...] += rs_recv[other].astype(f32)
    total = own[...].astype(bf16)
    spread = lax.dot_general(selector, total, over_rows, preferred_element_type=f32).astype(bf16)
    kr_out[...] = spread
    for zd in range(planes):
        part = spread[zd * group * ROWS : (zd + 1) * group * ROWS]
        eg_send[zd] = (
            lax.dot_general(part[:, :width], wk_ref[...], over_cols, preferred_element_type=f32)
            + lax.dot_general(part[:, width:], wv_ref[...], over_cols, preferred_element_type=f32)
        ).astype(bf16)

    def member_rows(p):
        return eg_send.at[:, pl.ds(pl.multiple_of(p * ROWS, ROWS), ROWS), :]

    for s in range(1, group):
        p = flipped(j, s, group)
        send(member_rows(p), eg_recv.at[j], eg_s.at[p], eg_r.at[j], z, p).start()
    term = member_rows(j)[...].astype(f32)
    for s in range(1, group):
        p = flipped(j, s, group)
        arrive(eg_recv.at[p], eg_r.at[p])
        term = term + eg_recv[p].astype(f32)
    eg2_send[...] = term.astype(bf16)
    for d in range(1, planes):
        other = (z + d) % planes
        send(eg2_send.at[other], eg2_recv.at[z], eg2_s.at[other], eg2_r.at[z], other, j).start()
    final = eg2_send[z].astype(f32)
    for d in range(1, planes):
        other = (z + d) % planes
        arrive(eg2_recv.at[other], eg2_r.at[other])
        final = final + eg2_recv[other].astype(f32)
    eg_out[...] = final.astype(bf16)

    for d in range(1, planes):
        other = (z + d) % planes
        arrive(encx_ref, enc1_s.at[d])
        arrive(kv.at[z], kv_s.at[d])
        arrive(rs_send.at[other], rs_s.at[other])
        arrive(eg2_send.at[other], eg2_s.at[other])
    for s in range(1, group):
        p = flipped(j, s, group)
        arrive(encbuf.at[:, j], enc2_s.at[s])
        arrive(qid_ref, qid_s.at[s])
        arrive(member_rows(p), eg_s.at[p])

    def drain(d, carry):
        def peer(s, c):
            p = flipped(j, s, group)
            arrive(qbuf.at[d, p], q_s.at[d, p])
            arrive(gbuf.at[d, p], g_s.at[d, p])
            arrive(dqbuf.at[d, p], dq_s.at[d, p])
            arrive(dq_out.at[:, columns(d, p)], dq_r.at[d, p])
            return c

        arrive(dq_out.at[:, columns(d, j)], dq_r.at[d, j])
        return lax.fori_loop(1, group, peer, carry)

    lax.fori_loop(0, planes, drain, 0)


def body(n, queries, out_grad, enc_states, w_key, w_value, dec_segments, enc_segments):
    key_weight = lax.all_gather(w_key, "dp", axis=0, tiled=True)
    value_weight = lax.all_gather(w_value, "dp", axis=0, tiled=True)
    bf16, f32 = jnp.bfloat16, jnp.float32
    group = 8 if n % 8 == 0 else 1
    planes = n // group
    tokens = queries.shape[0]
    own_rows, depth = enc_states.shape
    width = key_weight.shape[1]
    keys = n * own_rows
    padded = n * ROWS
    ids = jnp.broadcast_to(enc_segments.astype(bf16)[:, None], (own_rows, tokens))
    encx = jnp.pad(jnp.concatenate([enc_states, ids], axis=1), ((0, ROWS - own_rows), (0, 0)))
    qid = jnp.broadcast_to(dec_segments.astype(f32)[None, :], (8, tokens))
    row = jnp.arange(keys, dtype=jnp.int32)
    place = row // own_rows * ROWS + row % own_rows
    selector = (place[:, None] == jnp.arange(padded, dtype=jnp.int32)[None, :]).astype(bf16)
    vm = pl.BlockSpec(memory_space=pltpu.VMEM)
    hbm = pl.BlockSpec(memory_space=pl.ANY)
    dma = pltpu.SemaphoreType.DMA
    pairs = (planes, group)
    dq, spread, encoder, enc_grad = pl.pallas_call(
        functools.partial(kernel, planes, group),
        out_shape=(
            jax.ShapeDtypeStruct((tokens, n * width), bf16),
            jax.ShapeDtypeStruct((padded, 2 * width), bf16),
            jax.ShapeDtypeStruct((padded, depth), bf16),
            jax.ShapeDtypeStruct((ROWS, depth), bf16),
        ),
        in_specs=[hbm, hbm, vm, vm, hbm, hbm, hbm],
        out_specs=(hbm, vm, vm, vm),
        scratch_shapes=[
            pltpu.VMEM((depth, width), bf16),
            pltpu.VMEM((depth, width), bf16),
            pltpu.VMEM((keys, padded), bf16),
            dma((3,)),
            pltpu.VMEM((planes, group, ROWS, depth + tokens), bf16),
            pltpu.VMEM((planes, group, tokens, width), bf16),
            pltpu.VMEM((planes, group, tokens, width), bf16),
            pltpu.VMEM((group, 8, tokens), f32),
            pltpu.VMEM((planes, keys, 2 * width), bf16),
            pltpu.VMEM((keys, tokens), f32),
            pltpu.VMEM((planes, group, tokens, width), bf16),
            pltpu.VMEM((keys, 2 * width), f32),
            pltpu.VMEM((keys, 2 * width), f32),
            pltpu.VMEM((planes, keys, 2 * width), bf16),
            pltpu.VMEM((planes, keys, 2 * width), bf16),
            pltpu.VMEM((planes, group * ROWS, depth), bf16),
            pltpu.VMEM((group, planes, ROWS, depth), bf16),
            pltpu.VMEM((planes, ROWS, depth), bf16),
            pltpu.VMEM((planes, ROWS, depth), bf16),
            dma((planes,)), dma((planes,)), dma((group,)), dma((group,)),
            dma((group,)), dma((group,)),
            dma(pairs), dma(pairs), dma(pairs), dma(pairs),
            dma((planes,)), dma((planes,)), dma(pairs), dma(pairs),
            dma((planes,)), dma((planes,)), dma((group,)), dma((group,)),
            dma((planes,)), dma((planes,)),
        ],
        compiler_params=pltpu.CompilerParams(
            collective_id=0, has_side_effects=True, vmem_limit_bytes=48 * 1024 * 1024
        ),
    )(queries, out_grad, qid, encx, key_weight, value_weight, selector)
    down = (((0,), (0,)), ((), ()))
    grads = []
    for first in (0, width):
        term = lax.dot_general(
            encoder, spread[:, first : first + width], down, preferred_element_type=f32
        )
        if lax.axis_size("dp") > 1:
            term = lax.psum_scatter(
                term.astype(bf16), "dp", scatter_dimension=0, tiled=True
            ).astype(f32)
        grads.append(term)
    return dq, enc_grad[:own_rows], grads[0], grads[1]


def solution(mesh):
    both = ("dp", "ctx")
    in_specs = (
        P(both, None), P(both, None), P(both, None), P("dp", "ctx"), P("dp", "ctx"), P(both), P(both),
    )
    out_specs = (P(both, None), P(both, None), P("dp", "ctx"), P("dp", "ctx"))
    return jax.shard_map(
        functools.partial(body, mesh.shape["ctx"]),
        mesh=mesh, in_specs=in_specs, out_specs=out_specs, check_vma=False,
    )
```
